32 devices in a mesh: expert: 16 (over z, y, x), dp: 2 (over core).
Axes of the slice: x: 2, y: 2, z: 4, core: 2. Of those that a mesh axis runs over, the one named last changes fastest.
Arguments:
- tokens: bfloat16 [768, 2048], P(('expert', 'dp')), may hold values from -6 to 6
- cotangent: bfloat16 [768, 2048], P(('expert', 'dp')), may hold values from -6 to 6
- route_gates: bfloat16 [768, 6], P(('expert', 'dp')), may hold values from 0.049804688 to 1
- routes: int32 [768, 6], P(('expert', 'dp')), may hold values from 0 to 15, all different within a row; in each aligned block of 24 rows (0 to 23, 24 to 47, ...) at most 12 rows name the same one
- w_gate: bfloat16 [16, 1408, 2048], P('expert', 'dp'), may hold values from -0.125 to 0.125
- w_up: bfloat16 [16, 1408, 2048], P('expert', 'dp'), may hold values from -0.125 to 0.125
- w_down: bfloat16 [16, 1408, 2048], P('expert', 'dp'), may hold values from -0.15625 to 0.15625
Outputs:
- layer_out: bfloat16 [768, 2048], P(('expert', 'dp'))
- token_grad: bfloat16 [768, 2048], P(('expert', 'dp'))
- gate_grad: float32 [768, 6], P(('expert', 'dp'))
- grad_gate_proj: float32 [16, 1408, 2048], P('expert', 'dp')
- grad_up_proj: float32 [16, 1408, 2048], P('expert', 'dp')
- grad_down_proj: float32 [16, 1408, 2048], P('expert', 'dp')
The draws below stay inside these ranges and needn't reach their ends.
Inputs may be any that keep to these rules, and one draw needn't show every extreme that they name: `routes`: each row names 6 different experts. In the rows of one device no expert is named by more than 12 rows.
All inputs are finite; a program needn't handle non-finite values.
Results may differ from the reference program's by a relative error of at most 0.01.
Values may be sent and summed in bfloat16 or wider, within the bound.
A program may use at most 128 MiB of HBM per device.

```python
import math
import jax
import jax.numpy as jnp
import numpy as np
from jax import lax

D = 2048
FF = 1408
TOPK = 6
TOK_DEV = 24
EXPERTS = 16
CAP = 12
TOKENS = 768
N_DP = 2


def shard_levels(stream_key, shape, cuts, low, top_value):
    gain, own = 1.0, jax.random.fold_in(stream_key, 6)
    for dim, blocks in cuts:
        draws = jnp.exp(jax.random.uniform(jax.random.fold_in(own, dim), (blocks,), jnp.float32, low / len(cuts), top_value / len(cuts)))
        gain = gain * jnp.repeat(draws, shape[dim] // blocks).reshape([-1 if axis == dim else 1 for axis in range(len(shape))])
    return gain


def routed_block(stream_key, own, number, rows, amount, top, most, lean):
    ranking = jax.random.permutation(stream_key, amount)
    heavy_load, ordinary = load_shares(amount, rows * top, most, lean, True), load_shares(amount, rows * top, most, lean, False)
    places = jnp.arange(amount)

    def named(lengths, offset_by):
        used = int((lengths > 0).sum())
        fixed = max(1, used // 4)
        passed = fixed + (places - fixed + offset_by * (used - fixed)) % max(1, amount - fixed)
        return jnp.zeros((amount,), jnp.int32).at[ranking[jnp.where(places < fixed, places, passed)]].set(jnp.asarray(lengths, jnp.int32))

    lengths = jnp.where(number % 4 == 0, named(heavy_load, number // 4), named(ordinary, number - number // 4 - 1))
    mixed = jax.random.permutation(jax.random.fold_in(own, 3), amount)
    giver, taker = mixed[0:amount // 2 * 2:2], mixed[1:amount // 2 * 2:2]
    slack = jnp.minimum(lengths[giver] - 1, most - lengths[taker]) // 2
    slack = jnp.where((giver == ranking[0]) | (taker == ranking[0]) | (lengths[taker] == 0), 0, jnp.maximum(slack, 0))
    passed = jax.random.randint(jax.random.fold_in(own, 4), (amount // 2,), 0, 1 << 20) % (slack + 1)
    lengths = lengths.at[giver].add(-passed).at[taker].add(passed)
    labels = jnp.searchsorted(jnp.cumsum(lengths), jnp.arange(rows * top), side="right").astype(jnp.int32)
    table = labels.reshape(top, rows).T
    table = table[jax.random.permutation(jax.random.fold_in(own, 1), rows)]
    offset_by = jax.random.randint(jax.random.fold_in(own, 2), (rows, 1), 0, top)
    return jnp.take_along_axis(table, (jnp.arange(top)[None, :] + offset_by) % top, axis=1)


def load_shares(count, total, bound, slope, full):
    loads = [(1 << 20) // math.isqrt(standing ** slope) + 1 for standing in range(1, count + 1)]
    largest = bound if full else min(bound, max(-(-total // count), total * loads[0] // sum(loads)))
    least = 1 if total - largest >= count - 1 else 0
    counts, surplus = [largest] + [least] * (count - 1), total - largest - least * (count - 1)
    while surplus > 0:
        movable = [i for i in range(1, count) if counts[i] < largest] or [i for i in range(1, count) if counts[i] < bound]
        mass, left = sum([loads[i] for i in movable]), surplus
        for i in movable:
            extra = min(bound - counts[i], max(1, left * loads[i] // mass), surplus)
            counts[i] = counts[i] + extra
            surplus = surplus - extra
    return np.array(counts)


def gaussian(stream_key, extent, scale, reach, pieces=(), kind=jnp.bfloat16):
    drawn = scale * jax.random.normal(stream_key, extent, jnp.float32)
    if pieces:
        drawn = drawn * shard_levels(stream_key, extent, pieces, -0.22, 0.18)
    return jnp.clip(drawn, -reach, reach).astype(kind)


def setup_inputs(seed: int = 0) -> dict:
    seeds = jax.random.split(jax.random.key(seed), 8)
    tokens = gaussian(seeds[0], (TOKENS, D), 1.0, 6.0, ((0, 32),))
    cotangent = gaussian(seeds[1], (TOKENS, D), 1.0, 6.0, ((0, 32),))
    route_gates = jnp.clip(jnp.exp(math.log(1.0) - 2.9996462 * jax.random.uniform(seeds[2], (TOKENS, TOPK), jnp.float32) ** shard_levels(seeds[2], (TOKENS, TOPK), ((0, 32),), -0.2, 0.2)), 0.049804688, 1.0).astype(jnp.bfloat16)
    routes_keys = jax.random.split(jax.random.fold_in(seeds[3], 1), TOKENS // TOK_DEV)
    routes_turns = jax.random.permutation(jax.random.fold_in(seeds[3], 3), TOKENS // TOK_DEV)
    routes = jax.vmap(lambda own, number: routed_block(jax.random.fold_in(seeds[3], 2), own, number, TOK_DEV, EXPERTS, TOPK, CAP, 2))(routes_keys, routes_turns).reshape((TOKENS, TOPK))
    w_gate = gaussian(seeds[4], (EXPERTS, FF, D), D ** -0.5, 0.125, ((0, 16), (1, 2)))
    w_up = gaussian(seeds[5], (EXPERTS, FF, D), D ** -0.5, 0.125, ((0, 16), (1, 2)))
    w_down = gaussian(seeds[6], (EXPERTS, FF, D), FF ** -0.5, 0.15625, ((0, 16), (1, 2)))
    return dict(tokens=tokens, cotangent=cotangent, route_gates=route_gates, routes=routes, w_gate=w_gate, w_up=w_up, w_down=w_down)


def expert_rows(rows_in, rows_back, gate_proj, up_proj, down_proj):
    row_count = rows_in.shape[0]
    hidden_shard = FF // N_DP
    inner = (((1,), (1,)), ((), ()))
    outer = (((0,), (0,)), ((), ()))
    gate_pre = lax.dot_general(rows_in, gate_proj, inner, preferred_element_type=jnp.float32)
    up_pre = lax.dot_general(rows_in, up_proj, inner, preferred_element_type=jnp.float32)
    sigmoid_gate = jax.nn.sigmoid(gate_pre)
    hidden = (gate_pre * sigmoid_gate * up_pre).astype(jnp.bfloat16)
    parts = jnp.einsum("rjf,jfd->rjd", hidden.astype(jnp.float32).reshape(row_count, N_DP, hidden_shard),
                       down_proj.astype(jnp.float32).reshape(N_DP, hidden_shard, D)).astype(jnp.bfloat16)
    summed_out = jnp.sum(parts.astype(jnp.float32), axis=1)
    back_hidden = jnp.dot(rows_back, down_proj.T, preferred_element_type=jnp.float32)
    grad_pre = (back_hidden * up_pre * sigmoid_gate * (1.0 + gate_pre * (1.0 - sigmoid_gate))).astype(jnp.bfloat16)
    grad_upv = (back_hidden * gate_pre * sigmoid_gate).astype(jnp.bfloat16)
    grad_down = jnp.dot(hidden.T, rows_back, preferred_element_type=jnp.float32)
    grad_gate = lax.dot_general(grad_pre, rows_in, outer, preferred_element_type=jnp.float32)
    grad_up = lax.dot_general(grad_upv, rows_in, outer, preferred_element_type=jnp.float32)
    token_parts = jnp.einsum("rjf,jfd->rjd", grad_pre.astype(jnp.float32).reshape(row_count, N_DP, hidden_shard),
                             gate_proj.astype(jnp.float32).reshape(N_DP, hidden_shard, D))
    token_parts = token_parts + jnp.einsum("rjf,jfd->rjd", grad_upv.astype(jnp.float32).reshape(row_count, N_DP, hidden_shard),
                                           up_proj.astype(jnp.float32).reshape(N_DP, hidden_shard, D))
    summed_back = jnp.sum(token_parts.astype(jnp.bfloat16).astype(jnp.float32), axis=1)
    return summed_out, summed_back, grad_gate, grad_up, grad_down


def reference(tokens, cotangent, route_gates, routes, w_gate, w_up, w_down):
    token_count = tokens.shape[0]
    blocks = token_count // TOK_DEV
    per_block = TOK_DEV * TOPK
    flat_routes = routes.reshape(blocks, per_block)
    onehot = (flat_routes[:, :, None] == jnp.arange(EXPERTS, dtype=jnp.int32)[None, None, :]).astype(jnp.int32)
    before = jnp.cumsum(onehot, axis=1) - onehot
    slot_rank = jnp.sum(before * onehot, axis=2)
    block_ids = jnp.arange(blocks, dtype=jnp.int32)[:, None]
    target = (flat_routes * blocks + block_ids) * CAP + slot_rank
    source = jnp.arange(token_count * TOPK, dtype=jnp.int32).reshape(blocks, per_block)
    sentinel = token_count * TOPK
    slot_source = jnp.full((EXPERTS * blocks * CAP,), sentinel, dtype=jnp.int32)
    slot_source = slot_source.at[target.reshape(-1)].set(source.reshape(-1)).reshape(EXPERTS, blocks * CAP)
    token_table = jnp.concatenate([tokens, jnp.zeros((1, D), tokens.dtype)], axis=0)
    scaled = (route_gates.astype(jnp.float32)[:, :, None] * cotangent.astype(jnp.float32)[:, None, :]).astype(jnp.bfloat16)
    scaled_table = jnp.concatenate([scaled.reshape(token_count * TOPK, D), jnp.zeros((1, D), scaled.dtype)], axis=0)

    def per_expert(operands):
        slot_ids, gate_proj, up_proj, down_proj = operands
        return expert_rows(token_table[slot_ids // TOPK], scaled_table[slot_ids], gate_proj, up_proj, down_proj)

    summed_out, summed_back, grad_gate, grad_up, grad_down = lax.map(per_expert, (slot_source, w_gate, w_up, w_down))
    flat_ids = slot_source.reshape(-1)
    route_out = jnp.zeros((token_count * TOPK + 1, D), jnp.float32).at[flat_ids].set(summed_out.reshape(-1, D))
    route_out = route_out[:-1].reshape(token_count, TOPK, D)
    route_back = jnp.zeros((token_count * TOPK + 1, D), jnp.float32).at[flat_ids].set(summed_back.reshape(-1, D))
    route_back = route_back[:-1].reshape(token_count, TOPK, D)
    layer_out = jnp.sum(route_gates.astype(jnp.float32)[:, :, None] * route_out, axis=1).astype(jnp.bfloat16)
    gate_grad = jnp.sum(cotangent.astype(jnp.float32)[:, None, :] * route_out, axis=2)
    token_grad = jnp.sum(route_back, axis=1).astype(jnp.bfloat16)
    return (layer_out, token_grad, gate_grad, grad_gate, grad_up, grad_down)
```

```python
import jax
import jax.numpy as jnp
from jax import lax
from jax.sharding import PartitionSpec as P

AXES = ("expert", "dp")
INNER = (((1,), (1,)), ((), ()))
OUTER = (((0,), (0,)), ((), ()))


def dot_f32(left, right, dims=(((1,), (0,)), ((), ()))):
    return lax.dot_general(left, right, dims, preferred_element_type=jnp.float32)


def per_device(tokens, cotangent, route_gates, routes, w_gate, w_up, w_down):
    experts = lax.axis_size("expert")
    blocks = experts * lax.axis_size("dp")
    token_count, top_count = routes.shape
    capacity = max(2, token_count * top_count * 4 // (3 * experts))
    total = blocks * token_count
    slots = blocks * capacity
    gate_shard, up_shard, down_shard = (w_gate[0], w_up[0], w_down[0])
    me = lax.axis_index("expert")

    routing = jnp.concatenate(
        [routes.astype(jnp.float32), route_gates.astype(jnp.float32)], axis=1
    )
    routing = lax.all_gather(routing, AXES, axis=0, tiled=True)
    all_tokens = lax.all_gather(tokens, AXES, axis=0, tiled=True)
    all_cot = lax.all_gather(cotangent, AXES, axis=0, tiled=True)

    match = (routing[:, :top_count] == me.astype(jnp.float32)).astype(jnp.float32)
    gates = jnp.sum(match * routing[:, top_count:], axis=1)
    used = jnp.sum(match, axis=1)
    used_blocks = used.reshape(blocks, token_count)
    order = jnp.arange(token_count, dtype=jnp.int32)
    lower = (order[:, None] < order[None, :]).astype(jnp.bfloat16)
    rank = dot_f32(used_blocks.astype(jnp.bfloat16), lower)
    base = (jnp.arange(blocks, dtype=jnp.int32) * capacity).astype(jnp.float32)
    slot = jnp.where(used_blocks > 0, rank + base[:, None], -1.0).reshape(total)
    slot_ids = jnp.arange(slots, dtype=jnp.int32).astype(jnp.float32)
    hit = slot_ids[:, None] == slot[None, :]
    pick = hit.astype(jnp.bfloat16)
    weigh = jnp.where(hit, gates[None, :], 0.0).astype(jnp.bfloat16)
    row_gate = jnp.sum(jnp.where(hit, gates[None, :], 0.0), axis=1)

    rows_in = dot_f32(pick, all_tokens).astype(jnp.bfloat16)
    gate_pre = dot_f32(rows_in, gate_shard, INNER)
    up_pre = dot_f32(rows_in, up_shard, INNER)
    sig = jax.nn.sigmoid(gate_pre)
    hidden = (gate_pre * sig * up_pre).astype(jnp.bfloat16)
    out_part = dot_f32(hidden, down_shard).astype(jnp.bfloat16)
    mixed = dot_f32(weigh, out_part, OUTER).astype(jnp.bfloat16)
    mixed = lax.psum_scatter(mixed, AXES, scatter_dimension=0, tiled=True)

    cot_rows = dot_f32(pick, all_cot)
    row_grad = jnp.sum(cot_rows * out_part.astype(jnp.float32), axis=1)
    rows_back = (cot_rows * row_gate[:, None]).astype(jnp.bfloat16)
    token_gg = jnp.sum(jnp.where(hit, row_grad[:, None], 0.0), axis=0)
    gate_grad = lax.psum_scatter(
        match * token_gg[:, None], AXES, scatter_dimension=0, tiled=True
    )
    back_hidden = dot_f32(rows_back, down_shard, INNER)
    grad_pre = (back_hidden * up_pre * sig * (1.0 + gate_pre * (1.0 - sig))).astype(jnp.bfloat16)
    grad_upv = (back_hidden * gate_pre * sig).astype(jnp.bfloat16)
    back_part = (dot_f32(grad_pre, gate_shard) + dot_f32(grad_upv, up_shard)).astype(jnp.bfloat16)
    token_grad = dot_f32(pick, back_part, OUTER).astype(jnp.bfloat16)
    token_grad = lax.psum_scatter(token_grad, AXES, scatter_dimension=0, tiled=True)
    grad_down = dot_f32(hidden, rows_back, OUTER)
    grad_gate = dot_f32(grad_pre, rows_in, OUTER)
    grad_up = dot_f32(grad_upv, rows_in, OUTER)
    return (mixed, token_grad, gate_grad, grad_gate[None], grad_up[None], grad_down[None])


def solution(mesh):
    row = P(("expert", "dp"), None)
    wide = P("expert", "dp", None)
    return jax.shard_map(
        per_device,
        mesh=mesh,
        in_specs=(row, row, row, row, wide, wide, wide),
        out_specs=(row, row, row, wide, wide, wide),
        check_vma=False,
    )
```

```python
import functools

import jax
import jax.numpy as jnp
from jax import lax
from jax.experimental import pallas as pl
from jax.experimental.pallas import tpu as pltpu
from jax.sharding import PartitionSpec as P

INNER = (((1,), (1,)), ((), ()))
OUTER = (((0,), (0,)), ((), ()))


def dot_f32(left, right, dims=(((1,), (0,)), ((), ()))):
    return lax.dot_general(left, right, dims, preferred_element_type=jnp.float32)


def gather_kernel(depth, group, *refs):
    ins, outs = refs[:3], refs[3:6]
    own_sem, send_sem, recv_sem = refs[6:]
    me, core = lax.axis_index("expert"), lax.axis_index("dp")
    z, y, x = me // 4, (me // 2) % 2, me % 2

    def at(zz, yy, xx, cc):
        return (zz * 4 + yy * 2 + xx, cc)

    deep = [at((z + k) % depth, y, x, core) for k in range(1, depth)]
    across, beside = at(z, 1 - y, x, core), at(z, y, 1 - x, core)
    mates = [at(z, y, x, (core + k) % group) for k in range(1, group)]
    peers = deep + [across, beside] + mates
    barrier = pltpu.get_barrier_semaphore()
    for peer in peers:
        pl.semaphore_signal(barrier, inc=1, device_id=peer, device_id_type=pl.DeviceIdType.MESH)
    pl.semaphore_wait(barrier, len(peers))

    sent, used = [], [0]

    def push(src, dst, peer):
        index = used[0]
        used[0] += 1
        copy = pltpu.make_async_remote_copy(
            src_ref=src, dst_ref=dst, send_sem=send_sem.at[index], recv_sem=recv_sem.at[index],
            device_id=peer, device_id_type=pl.DeviceIdType.MESH,
        )
        copy.start()
        sent.append(copy)
        return copy

    def arrived(copies):
        for copy in copies:
            copy.wait_recv()

    def share(view):
        return [push(view, view, peer) for peer in mates]

    def pieces(t):
        width = ins[t].shape[1]
        half = width // 2 if width % 256 == 0 else width
        return half, [pl.ds(0, half)] + ([pl.ds(half, width - half)] if half < width else [])

    own = []
    for t in range(3):
        copy = pltpu.make_async_copy(ins[t], outs[t].at[z, y, x, core], own_sem.at[t])
        copy.start()
        own.append(copy)

    def first(t):
        return [push(ins[t], outs[t].at[z, y, x, core], peer) for peer in deep]

    def second(t):
        moved = []
        for i, cols in enumerate(pieces(t)[1]):
            view = outs[t].at[:, y, x, core, :, cols]
            moved.append(push(view, view, across if i == 0 else beside))
        return moved, share(outs[t].at[:, y, x, core])

    def third(t):
        moved, shared = [], []
        for i, cols in enumerate(pieces(t)[1]):
            if i == 0:
                view, new = outs[t].at[:, :, x, core, :, cols], outs[t].at[:, 1 - y, x, core, :, cols]
            else:
                view, new = outs[t].at[:, y, :, core, :, cols], outs[t].at[:, y, 1 - x, core, :, cols]
            moved.append(push(view, view, beside if i == 0 else across))
            shared += share(new)
        return moved, shared

    def last(t):
        shared = []
        for i, cols in enumerate(pieces(t)[1]):
            new = outs[t].at[:, :, 1 - x, core, :, cols] if i == 0 else outs[t].at[:, 1 - y, :, core, :, cols]
            shared += share(new)
        return shared

    pending = []
    step_m, step_a = first(0), first(1)
    for copy in own:
        copy.wait()
    arrived(step_m)
    step_m, shared = second(0)
    pending += shared
    arrived(step_a)
    step_a, shared = second(1)
    pending += shared
    step_b = first(2)
    arrived(step_m)
    step_m, shared = third(0)
    pending += shared
    arrived(step_a)
    step_a, shared = third(1)
    pending += shared
    arrived(step_b)
    step_b, shared = second(2)
    pending += shared
    arrived(step_m)
    pending += last(0)
    arrived(step_a)
    pending += last(1)
    arrived(step_b)
    step_b, shared = third(2)
    pending += shared
    arrived(step_b)
    pending += last(2)
    arrived(pending)
    for copy in sent:
        copy.wait_send()


def gather_all(experts, group, arrays):
    depth = experts // 4
    copies = 3 * (depth + 9 + 5 * group)
    shapes = [
        jax.ShapeDtypeStruct((depth, 2, 2, group) + array.shape, array.dtype) for array in arrays
    ]
    outs = pl.pallas_call(
        functools.partial(gather_kernel, depth, group),
        out_shape=shapes,
        in_specs=[pl.BlockSpec(memory_space=pltpu.VMEM)] * 3,
        out_specs=[pl.BlockSpec(memory_space=pl.ANY)] * 3,
        scratch_shapes=[
            pltpu.SemaphoreType.DMA((3,)),
            pltpu.SemaphoreType.DMA((copies,)),
            pltpu.SemaphoreType.DMA((copies,)),
        ],
        compiler_params=pltpu.CompilerParams(collective_id=0, has_side_effects=True),
    )(*arrays)
    return [out.reshape(-1, out.shape[-1]) for out in outs]


def per_device(tokens, cotangent, route_gates, routes, w_gate, w_up, w_down):
    experts, group = lax.axis_size("expert"), lax.axis_size("dp")
    blocks = experts * group
    token_count, top_count = routes.shape
    width = tokens.shape[1]
    capacity = max(2, token_count * top_count * 4 // (3 * experts))
    total, slots, sent = blocks * token_count, blocks * capacity, experts * capacity
    gate_shard, up_shard, down_shard = (w_gate[0], w_up[0], w_down[0])
    me = lax.axis_index("expert")

    routing = jnp.concatenate([routes.astype(jnp.bfloat16), route_gates], axis=1)
    routing = jnp.pad(routing, ((0, 0), (0, 128 - 2 * top_count)))
    routing, all_tokens, all_cot = gather_all(experts, group, [routing, tokens, cotangent])
    routing = routing[:, : 2 * top_count].astype(jnp.float32)

    match = (routing[:, :top_count] == me.astype(jnp.float32)).astype(jnp.float32)
    gates = jnp.sum(match * routing[:, top_count:], axis=1)
    used = jnp.sum(match, axis=1).reshape(blocks, token_count)
    order = jnp.arange(token_count, dtype=jnp.int32)
    lower = (order[:, None] < order[None, :]).astype(jnp.bfloat16)
    rank = dot_f32(used.astype(jnp.bfloat16), lower)
    number = jnp.arange(blocks, dtype=jnp.int32)
    base = ((number % group) * experts + number // group) * capacity
    slot = jnp.where(used > 0, rank + base.astype(jnp.float32)[:, None], -1.0).reshape(total)
    slot_ids = jnp.arange(slots, dtype=jnp.int32).astype(jnp.float32)
    hit = slot_ids[:, None] == slot[None, :]
    pick = hit.astype(jnp.bfloat16)
    row_gate = jnp.sum(jnp.where(hit, gates[None, :], 0.0), axis=1)

    expert_ids = jnp.arange(experts, dtype=jnp.int32)
    named = routes[:, :, None] == expert_ids[None, None, :]
    mine = jnp.sum(named.astype(jnp.int32), axis=1)
    place = jnp.cumsum(mine, axis=0) - mine + expert_ids[None, :] * capacity
    route_slot = jnp.sum(jnp.where(named, place[:, None, :], 0), axis=2)
    taken = route_slot[:, :, None] == jnp.arange(sent, dtype=jnp.int32)[None, None, :]
    token_table = jnp.sum(taken.astype(jnp.float32), axis=1).astype(jnp.bfloat16)
    gate_table = jnp.sum(
        jnp.where(taken, route_gates.astype(jnp.float32)[:, :, None], 0.0), axis=1
    ).astype(jnp.bfloat16)
    own_cot = dot_f32(token_table, cotangent, OUTER)

    def send_home(part):
        part = lax.psum_scatter(
            part.reshape(group, sent, width), "dp", scatter_dimension=0, tiled=True
        )
        part = part.reshape(experts, capacity, width)
        part = lax.all_to_all(part, "expert", split_axis=0, concat_axis=0, tiled=True)
        return part.reshape(sent, width)

    rows_in = dot_f32(pick, all_tokens).astype(jnp.bfloat16)
    gate_pre = dot_f32(rows_in, gate_shard, INNER)
    up_pre = dot_f32(rows_in, up_shard, INNER)
    sig = jax.nn.sigmoid(gate_pre)
    hidden = (gate_pre * sig * up_pre).astype(jnp.bfloat16)
    back_out = send_home(dot_f32(hidden, down_shard).astype(jnp.bfloat16))
    rows_back = (dot_f32(pick, all_cot) * row_gate[:, None]).astype(jnp.bfloat16)
    back_hidden = dot_f32(rows_back, down_shard, INNER)
    grad_pre = (back_hidden * up_pre * sig * (1.0 + gate_pre * (1.0 - sig))).astype(jnp.bfloat16)
    grad_upv = (back_hidden * gate_pre * sig).astype(jnp.bfloat16)
    back_part = (dot_f32(grad_pre, gate_shard) + dot_f32(grad_upv, up_shard)).astype(jnp.bfloat16)
    back_grad = send_home(back_part)
    grad_down = dot_f32(hidden, rows_back, OUTER)
    grad_gate = dot_f32(grad_pre, rows_in, OUTER)
    grad_up = dot_f32(grad_upv, rows_in, OUTER)

    mixed = dot_f32(gate_table, back_out).astype(jnp.bfloat16)
    token_grad = dot_f32(token_table, back_grad).astype(jnp.bfloat16)
    row_grad = jnp.sum(own_cot * back_out.astype(jnp.float32), axis=1)
    gate_grad = jnp.sum(jnp.where(taken, row_grad[None, None, :], 0.0), axis=2)
    return (mixed, token_grad, gate_grad, grad_gate[None], grad_up[None], grad_down[None])


def solution(mesh):
    row = P(("expert", "dp"), None)
    wide = P("expert", "dp", None)
    return jax.shard_map(
        per_device,
        mesh=mesh,
        in_specs=(row, row, row, row, wide, wide, wide),
        out_specs=(row, row, row, wide, wide, wide),
        check_vma=False,
    )
```

```python
import functools

import jax
import jax.numpy as jnp
from jax import lax
from jax.experimental import pallas as pl
from jax.experimental.pallas import tpu as pltpu
from jax.sharding import PartitionSpec as P


INNER = (((1,), (1,)), ((), ()))
OUTER = (((0,), (0,)), ((), ()))


def dot_f32(left, right, dims=(((1,), (0,)), ((), ()))):
    return lax.dot_general(left, right, dims, preferred_element_type=jnp.float32)


def gather_kernel(depth, group, *refs):
    ins, outs = refs[:3], refs[3:6]
    own_sem, send_sem, recv_sem = refs[6:]
    me, core = lax.axis_index("expert"), lax.axis_index("dp")
    z, y, x = me // 4, (me // 2) % 2, me % 2

    def at(zz, yy, xx, cc):
        return (zz * 4 + yy * 2 + xx, cc)

    deep = [at((z + k) % depth, y, x, core) for k in range(1, depth)]
    across, beside = at(z, 1 - y, x, core), at(z, y, 1 - x, core)
    mates = [at(z, y, x, (core + k) % group) for k in range(1, group)]
    peers = deep + [across, beside] + mates
    barrier = pltpu.get_barrier_semaphore()
    for peer in peers:
        pl.semaphore_signal(barrier, inc=1, device_id=peer, device_id_type=pl.DeviceIdType.MESH)
    pl.semaphore_wait(barrier, len(peers))

    sent, used = [], [0]

    def push(src, dst, peer):
        index = used[0]
        used[0] += 1
        copy = pltpu.make_async_remote_copy(
            src_ref=src, dst_ref=dst, send_sem=send_sem.at[index], recv_sem=recv_sem.at[index],
            device_id=peer, device_id_type=pl.DeviceIdType.MESH,
        )
        copy.start()
        sent.append(copy)
        return copy

    def arrived(copies):
        for copy in copies:
            copy.wait_recv()

    def share(view):
        return [push(view, view, peer) for peer in mates]

    def pieces(t):
        width = ins[t].shape[1]
        half = width // 2 if width % 256 == 0 else width
        return half, [pl.ds(0, half)] + ([pl.ds(half, width - half)] if half < width else [])

    own = []
    for t in range(3):
        copy = pltpu.make_async_copy(ins[t], outs[t].at[z, y, x, core], own_sem.at[t])
        copy.start()
        own.append(copy)

    def first(t):
        return [push(ins[t], outs[t].at[z, y, x, core], peer) for peer in deep]

    def second(t):
        moved = []
        for i, cols in enumerate(pieces(t)[1]):
            view = outs[t].at[:, y, x, core, :, cols]
            moved.append(push(view, view, across if i == 0 else beside))
        return moved, share(outs[t].at[:, y, x, core])

    def third(t):
        moved, shared = [], []
        for i, cols in enumerate(pieces(t)[1]):
            if i == 0:
                view, new = outs[t].at[:, :, x, core, :, cols], outs[t].at[:, 1 - y, x, core, :, cols]
            else:
                view, new = outs[t].at[:, y, :, core, :, cols], outs[t].at[:, y, 1 - x, core, :, cols]
            moved.append(push(view, view, beside if i == 0 else across))
            shared += share(new)
        return moved, shared

    def last(t):
        shared = []
        for i, cols in enumerate(pieces(t)[1]):
            new = outs[t].at[:, :, 1 - x, core, :, cols] if i == 0 else outs[t].at[:, 1 - y, :, core, :, cols]
            shared += share(new)
        return shared

    pending = []
    step_m, step_a = first(0), first(1)
    for copy in own:
        copy.wait()
    arrived(step_m)
    step_m, shared = second(0)
    pending += shared
    arrived(step_a)
    step_a, shared = second(1)
    pending += shared
    step_b = first(2)
    arrived(step_m)
    step_m, shared = third(0)
    pending += shared
    arrived(step_a)
    step_a, shared = third(1)
    pending += shared
    arrived(step_b)
    step_b, shared = second(2)
    pending += shared
    arrived(step_m)
    pending += last(0)
    arrived(step_a)
    pending += last(1)
    arrived(step_b)
    step_b, shared = third(2)
    pending += shared
    arrived(step_b)
    pending += last(2)
    arrived(pending)
    for copy in sent:
        copy.wait_send()


def gather_all(experts, group, arrays):
    depth = experts // 4
    copies = 3 * (depth + 9 + 5 * group)
    shapes = [
        jax.ShapeDtypeStruct((depth, 2, 2, group) + array.shape, array.dtype) for array in arrays
    ]
    outs = pl.pallas_call(
        functools.partial(gather_kernel, depth, group),
        out_shape=shapes,
        in_specs=[pl.BlockSpec(memory_space=pltpu.VMEM)] * 3,
        out_specs=[pl.BlockSpec(memory_space=pl.ANY)] * 3,
        scratch_shapes=[
            pltpu.SemaphoreType.DMA((3,)),
            pltpu.SemaphoreType.DMA((copies,)),
            pltpu.SemaphoreType.DMA((copies,)),
        ],
        compiler_params=pltpu.CompilerParams(collective_id=0, has_side_effects=True),
    )(*arrays)
    return [out.reshape(-1, out.shape[-1]) for out in outs]


def per_device(tokens, cotangent, route_gates, routes, w_gate, w_up, w_down):
    experts, group = lax.axis_size("expert"), lax.axis_size("dp")
    blocks = experts * group
    token_count, top_count = routes.shape
    width = tokens.shape[1]
    capacity = max(2, token_count * top_count * 4 // (3 * experts))
    total, slots, sent = blocks * token_count, blocks * capacity, experts * capacity
    gate_shard, up_shard, down_shard = (w_gate[0], w_up[0], w_down[0])
    me = lax.axis_index("expert")

    routing = jnp.concatenate([routes.astype(jnp.bfloat16), route_gates], axis=1)
    routing = jnp.pad(routing, ((0, 0), (0, 128 - 2 * top_count)))
    routing, all_tokens, all_cot = gather_all(experts, group, [routing, tokens, cotangent])
    routing = routing[:, : 2 * top_count].astype(jnp.float32)

    match = (routing[:, :top_count] == me.astype(jnp.float32)).astype(jnp.float32)
    gates = jnp.sum(match * routing[:, top_count:], axis=1)
    used = jnp.sum(match, axis=1).reshape(blocks, token_count)
    order = jnp.arange(token_count, dtype=jnp.int32)
    lower = (order[:, None] < order[None, :]).astype(jnp.bfloat16)
    rank = dot_f32(used.astype(jnp.bfloat16), lower)
    number = jnp.arange(blocks, dtype=jnp.int32)
    base = ((number % group) * experts + number // group) * capacity
    slot = jnp.where(used > 0, rank + base.astype(jnp.float32)[:, None], -1.0).reshape(total)
    slot_ids = jnp.arange(slots, dtype=jnp.int32).astype(jnp.float32)
    hit = slot_ids[:, None] == slot[None, :]
    pick = hit.astype(jnp.bfloat16)
    row_gate = jnp.sum(jnp.where(hit, gates[None, :], 0.0), axis=1)

    expert_ids = jnp.arange(experts, dtype=jnp.int32)
    named = routes[:, :, None] == expert_ids[None, None, :]
    mine = jnp.sum(named.astype(jnp.int32), axis=1)
    place = jnp.cumsum(mine, axis=0) - mine + expert_ids[None, :] * capacity
    route_slot = jnp.sum(jnp.where(named, place[:, None, :], 0), axis=2)
    taken = route_slot[:, :, None] == jnp.arange(sent, dtype=jnp.int32)[None, None, :]
    token_table = jnp.sum(taken.astype(jnp.float32), axis=1).astype(jnp.bfloat16)
    gate_table = jnp.sum(
        jnp.where(taken, route_gates.astype(jnp.float32)[:, :, None], 0.0), axis=1
    ).astype(jnp.bfloat16)
    own_cot = dot_f32(token_table, cotangent, OUTER)

    def sum_halves(part):
        part = part.reshape(group, sent, width)
        return lax.psum_scatter(part, "dp", scatter_dimension=0, tiled=True)

    def send_home(part):
        part = part.reshape(experts, capacity, width)
        part = lax.all_to_all(part, "expert", split_axis=0, concat_axis=0, tiled=True)
        return part.reshape(sent, width)

    rows_in = dot_f32(pick, all_tokens).astype(jnp.bfloat16)
    gate_pre = dot_f32(rows_in, gate_shard, INNER)
    up_pre = dot_f32(rows_in, up_shard, INNER)
    sig = jax.nn.sigmoid(gate_pre)
    hidden = (gate_pre * sig * up_pre).astype(jnp.bfloat16)
    out_part = dot_f32(hidden, down_shard).astype(jnp.bfloat16)
    out_part, all_cot = lax.optimization_barrier((out_part, all_cot))
    out_sum = sum_halves(out_part)
    rows_back = (dot_f32(pick, all_cot) * row_gate[:, None]).astype(jnp.bfloat16)
    back_hidden = dot_f32(rows_back, down_shard, INNER)
    grad_pre = (back_hidden * up_pre * sig * (1.0 + gate_pre * (1.0 - sig))).astype(jnp.bfloat16)
    grad_upv = (back_hidden * gate_pre * sig).astype(jnp.bfloat16)
    out_sum, grad_pre, grad_upv = lax.optimization_barrier((out_sum, grad_pre, grad_upv))
    back_out = send_home(out_sum)
    back_part = (dot_f32(grad_pre, gate_shard) + dot_f32(grad_upv, up_shard)).astype(jnp.bfloat16)
    back_grad = send_home(sum_halves(back_part))
    grad_down = dot_f32(hidden, rows_back, OUTER)
    grad_gate = dot_f32(grad_pre, rows_in, OUTER)
    grad_up = dot_f32(grad_upv, rows_in, OUTER)

    mixed = dot_f32(gate_table, back_out).astype(jnp.bfloat16)
    token_grad = dot_f32(token_table, back_grad).astype(jnp.bfloat16)
    row_grad = jnp.sum(own_cot * back_out.astype(jnp.float32), axis=1)
    gate_grad = jnp.sum(jnp.where(taken, row_grad[None, None, :], 0.0), axis=2)
    return (mixed, token_grad, gate_grad, grad_gate[None], grad_up[None], grad_down[None])


def solution(mesh):
    row = P(("expert", "dp"), None)
    wide = P("expert", "dp", None)
    return jax.shard_map(
        per_device,
        mesh=mesh,
        in_specs=(row, row, row, row, wide, wide, wide),
        out_specs=(row, row, row, wide, wide, wide),
        check_vma=False,
    )
```
